32 devices in a mesh: gx: 16 (over z, x, core), gy: 2 (over y).
Axes of the slice: x: 2, y: 2, z: 4, core: 2. Of those that a mesh axis runs over, the one named last changes fastest.
Arguments:
- flexibility: bfloat16 [16, 2, 2048, 2048], P('gx', 'gy'), may hold values from -8 to 8
- loads: bfloat16 [16, 2, 192, 2048], P('gx', 'gy'), may hold values from -30 to 30
- dof_order: int32 [16, 2, 2048], P('gx', 'gy'), may hold values from 0 to 2047, each once within a row
- coarse_ids: int32 [16, 2, 128], P('gx', 'gy'), may hold values from 0 to 127, each once within a row
Outputs:
- field: float32 [16, 2, 192, 2048], P('gx', 'gy')
- multipliers: float32 [16, 2, 192, 2048], P('gx', 'gy')
The draws below stay inside these ranges and needn't reach their ends.
All inputs are finite; a program needn't handle non-finite values.
Results may differ from the reference program's by a relative error of at most 0.0038.
Values may be sent and summed in bfloat16 or wider, within the bound.
A program may use at most 64 MiB of HBM per device.

```python
import math
import jax
import jax.numpy as jnp
from jax import lax

ORDER = 2048
FACE = 320
CORN = 128
CPT = 32
RHS = 192
ITERS = 2
NSX = 16
NSY = 2


LOAD_LEVEL = 0.15


def draw_flexibility(key, part):
    first, second, third = jax.random.split(key, 3)
    keys = jax.random.split(first, NSX * NSY)
    diagonal = jax.random.uniform(second, (NSX * NSY, ORDER), jnp.float32, 1.5, 3.0)
    stiffness = jnp.exp(jax.random.uniform(third, (NSX * NSY,), jnp.float32, math.log(0.5), math.log(2.0)))
    eye = jnp.eye(ORDER, dtype=jnp.float32)

    def one_matrix(triple):
        base = jax.random.normal(triple[0], (ORDER, ORDER), jnp.float32)
        sym = (base + base.T) * (0.5 / math.sqrt(2.0 * ORDER))
        matrix = sym * (1.0 - eye) + triple[1][:, None] * eye
        return (matrix * triple[2]).astype(jnp.bfloat16)
    return lax.map(one_matrix, (keys, diagonal, stiffness)).reshape(NSX, NSY, ORDER, ORDER)


def draw_loads(key, part):
    first, second = jax.random.split(key, 2)
    ramp_x = jnp.exp(jnp.arange(NSX, dtype=jnp.float32) * (math.log(3.0) / (NSX - 1)))
    ramp_y = jnp.exp(jnp.arange(NSY, dtype=jnp.float32) * (math.log(3.0) / (NSY - 1)))
    ramp = ramp_x[:, None, None, None] * ramp_y[None, :, None, None]
    base = jnp.clip(jax.random.normal(first, (NSX, NSY, RHS, ORDER), jnp.float32), -4.0, 4.0)
    local = jnp.exp(jax.random.uniform(second, (NSX, NSY, 1, 1), jnp.float32, -math.log(4.0), math.log(4.0)))
    values = base * local
    return (values * ramp * LOAD_LEVEL).astype(jnp.bfloat16)


def setup_inputs(seed: int = 0) -> dict:
    key_of = jax.random.split(jax.random.key(seed), 5)
    flexibility = draw_flexibility(jax.random.fold_in(key_of[4], 71), 0)
    loads = draw_loads(jax.random.fold_in(key_of[4], 71), 0)
    dof_order = jax.vmap(lambda own: jax.random.permutation(own, ORDER))(jax.random.split(key_of[2], NSX * NSY)).reshape((NSX, NSY, ORDER)).astype(jnp.int32)
    coarse_ids = jax.vmap(lambda own: jax.random.permutation(own, CORN))(jax.random.split(key_of[3], NSX * NSY)).reshape((NSX, NSY, CORN)).astype(jnp.int32)
    return dict(flexibility=flexibility, loads=loads, dof_order=dof_order, coarse_ids=coarse_ids)


RHO = 0.2
RHO_CORNER = 0.5
EPS = 1e-06
ROUNDS = ((0, 1, 0), (0, 1, 1), (1, 1, 0), (1, 1, 1), (0, 2, 0), (0, 2, 2))

def partner_of(trace, axis, dist, offset):
    count = trace.shape[axis]
    index = jnp.arange(count)
    lower = (index - offset) // dist % 2 == 0
    above = jnp.roll(trace, -dist, axis)
    below = jnp.roll(trace, dist, axis)
    if axis == 0:
        above = jnp.where((index < count - dist)[:, None, None, None], above, jnp.zeros_like(above))
        below = jnp.where((index >= dist)[:, None, None, None], below, jnp.zeros_like(below))
        return jnp.where(lower[:, None, None, None], above, below)
    return jnp.where(lower[None, :, None, None], above, below)

def cross_averages(slotted):
    first = slotted[..., 0, :]
    second = slotted[..., 1, :]
    third = slotted[..., 2, :]
    fourth = slotted[..., 3, :]
    upper = first + jnp.roll(third, -1, axis=1)
    lower = second + jnp.roll(fourth, -1, axis=1)
    zero = jnp.zeros((1,) + first.shape[1:], jnp.float32)
    cross = jnp.concatenate([zero, upper], axis=0) + jnp.concatenate([lower, zero], axis=0)
    counts = jnp.full((NSX + 1,), 4.0, jnp.float32).at[0].set(2.0).at[NSX].set(2.0)
    means = cross / counts[:, None, None, None]
    slot_a = means[1:]
    slot_b = means[:-1]
    slot_c = jnp.roll(slot_a, 1, axis=1)
    slot_d = jnp.roll(slot_b, 1, axis=1)
    return jnp.stack([slot_a, slot_b, slot_c, slot_d], axis=3)

def reference(flexibility, loads, dof_order, coarse_ids):
    subs = NSX * NSY
    flat_flex = flexibility.reshape(subs, ORDER, ORDER)
    order_full = jnp.broadcast_to(dof_order[:, :, None, :], (NSX, NSY, RHS, ORDER))
    inverse = jnp.argsort(dof_order, axis=-1).astype(jnp.int32)
    inverse_full = jnp.broadcast_to(inverse[:, :, None, :], (NSX, NSY, RHS, ORDER))
    ids_full = jnp.broadcast_to(coarse_ids[:, :, None, :], (NSX, NSY, RHS, CORN))
    slot_inverse = jnp.argsort(coarse_ids, axis=-1).astype(jnp.int32)
    slot_full = jnp.broadcast_to(slot_inverse[:, :, None, :], (NSX, NSY, RHS, CORN))
    multipliers = jnp.zeros((NSX, NSY, RHS, ORDER), jnp.float32)
    field = multipliers
    for step in range(ITERS):
        rhs = (loads.astype(jnp.float32) - multipliers).astype(jnp.bfloat16)

        def solve_one(pair):
            return jnp.dot(pair[0], pair[1], preferred_element_type=jnp.float32)
        field = lax.map(solve_one, (rhs.reshape(subs, RHS, ORDER), flat_flex)).reshape(NSX, NSY, RHS, ORDER)
        ordered = jnp.take_along_axis(field, order_full, axis=3)
        pieces = []
        for r, (axis, dist, offset) in enumerate(ROUNDS):
            own = ordered[..., r * FACE:(r + 1) * FACE]
            other = partner_of(own.astype(jnp.bfloat16), axis, dist, offset)
            pieces.append(RHO * (own - other.astype(jnp.float32)))
        corners = ordered[..., 6 * FACE:]
        slotted = jnp.take_along_axis(corners, slot_full, axis=3).reshape(NSX, NSY, RHS, 4, CPT)
        averaged = cross_averages(slotted).reshape(NSX, NSY, RHS, CORN)
        average = jnp.take_along_axis(averaged, ids_full, axis=3)
        resid = corners - average
        msq = lax.optimization_barrier(jnp.sum(resid * resid, axis=(0, 1, 3))) / (NSX * NSY * CORN)
        scale = 1.0 / jnp.sqrt(msq + EPS)
        pieces.append(RHO_CORNER * resid * scale[None, None, :, None])
        update = jnp.concatenate(pieces, axis=3)
        multipliers = multipliers + jnp.take_along_axis(update, inverse_full, axis=3)
    return (field, multipliers)
```

```python
import functools
import jax
import jax.numpy as jnp
from jax import lax
from jax.experimental import pallas as pl
from jax.experimental.pallas import tpu as pltpu
from jax.sharding import PartitionSpec as P

ITERS = 2
RHO = 0.2
RHO_CORNER = 0.5
EPS = 1e-06
MESH = pl.DeviceIdType.MESH
ROUNDS = ((0, 1, 0), (0, 1, 1), (1, 1, 0), (1, 1, 1), (0, 2, 0), (0, 2, 2))
PAIRS = (2, 0, 1)
F32 = jnp.float32
BF16 = jnp.bfloat16


def dot(a, b):
    return jnp.dot(a, b, preferred_element_type=F32)


def dot_nt(a, b):
    return lax.dot_general(a, b, (((1,), (1,)), ((), ())), preferred_element_type=F32)


def split(x):
    hi = x.astype(BF16)
    return hi, (x - hi.astype(F32)).astype(BF16)


def fold(x, low):
    h = x.shape[0] // 2
    lane = lax.broadcasted_iota(jnp.int32, (h, 128), 1)
    top, bottom = x[:h], x[h:]
    if low:
        return jnp.where(lane < 64, top, pltpu.roll(bottom, 64, 1))
    return jnp.where(lane < 64, pltpu.roll(top, 64, 1), bottom)


def unfold(low, high):
    h = low.shape[0]
    lane = lax.broadcasted_iota(jnp.int32, (h, 128), 1)
    top = jnp.where(lane < 64, low, pltpu.roll(high, 64, 1))
    bottom = jnp.where(lane < 64, pltpu.roll(low, 64, 1), high)
    return jnp.concatenate([top, bottom], axis=0)


def kernel(nx, ny, order_ref, ids_ref, loads_ref, flex_hbm, field_out, mult_out,
           flex, perm, permt, cperm, cpermt, fld, fhi, flo, rhs, mult, cmask,
           tb, rv, cs, cr, us, ur, sq, sr,
           flex_sem, tsend, trecv, csend, crecv, usend, urecv, ssend, srecv, osem):
    rows, n = loads_ref.shape
    face = (n - 128) // 6
    pair_w = 2 * face
    ncorn = ids_ref.shape[1]
    nf = 6 * face
    ix, iy = lax.axis_index("gx"), lax.axis_index("gy")
    ndev = nx * ny
    me = ix * ny + iy
    nch = flex_sem.shape[0]
    cw = n // nch

    def flex_copy(c):
        s = pl.ds(c * cw, cw)
        return pltpu.make_async_copy(flex_hbm.at[:, s], flex.at[:, s], flex_sem.at[c])

    for c in range(nch):
        flex_copy(c).start()

    def peer(k):
        p = lax.rem(me + k, ndev)
        return (p // ny, lax.rem(p, ny))

    barrier = pltpu.get_barrier_semaphore()

    def greet(k, carry):
        pl.semaphore_signal(barrier, inc=1, device_id=peer(k), device_id_type=MESH)
        return carry

    lax.fori_loop(1, ndev, greet, 0)

    partners = []
    for axis, dist, off in ROUNDS:
        idx = ix if axis == 0 else iy
        count = nx if axis == 0 else ny
        lower = lax.rem((idx - off + 2 * dist) // dist, 2) == 0
        to = jnp.where(lower, idx + dist, idx - dist)
        if axis == 0:
            partners.append((jnp.logical_and(to >= 0, to < count), (jnp.clip(to, 0, count - 1), iy)))
        else:
            partners.append((None, (ix, lax.rem(to + count, count))))

    for it in range(ITERS):
        for r in range(6):
            present = partners[r][0]
            if present is not None:
                @pl.when(jnp.logical_not(present))
                def _():
                    rv[it, r] = jnp.zeros(rv.shape[2:], BF16)
        @pl.when(ix == 0)
        def _():
            ur[it, 0] = jnp.zeros(ur.shape[2:], F32)
        @pl.when(ix == nx - 1)
        def _():
            ur[it, 1] = jnp.zeros(ur.shape[2:], F32)

    step_p = 64

    def build(b, carry):
        base = pl.multiple_of(b * step_p, step_p)
        row = lax.broadcasted_iota(jnp.int32, (step_p, n), 0) + base
        perm[pl.ds(base, step_p), :] = jnp.where(row == order_ref[...], 1.0, 0.0).astype(BF16)
        return carry

    lax.fori_loop(0, n // step_p, build, 0)
    ids = ids_ref[...]
    slot = ids // (ncorn // 4)
    moved = jnp.where(slot == 1, 2, jnp.where(slot == 2, 1, slot))
    ids = moved * (ncorn // 4) + lax.rem(ids, ncorn // 4)
    place = jnp.where(lax.broadcasted_iota(jnp.int32, (ncorn, ncorn), 0) == ids, 1.0, 0.0).astype(BF16)
    cperm[...] = dot_nt(perm[:, nf:], place).astype(BF16)

    def build_t():
        eye = (lax.broadcasted_iota(jnp.int32, (128, 128), 0)
               == lax.broadcasted_iota(jnp.int32, (128, 128), 1))

        def body(b, carry):
            base = pl.multiple_of(b * 128, 128)
            part = order_ref[:, pl.ds(base, 128)].astype(F32)
            col = jnp.sum(jnp.where(eye, part, 0.0), axis=1, keepdims=True).astype(jnp.int32)
            hit = lax.broadcasted_iota(jnp.int32, (128, n), 1) == col
            permt[pl.ds(base, 128), :] = jnp.where(hit, 1.0, 0.0).astype(BF16)
            return carry

        lax.fori_loop(0, n // 128, body, 0)
        ct = dot(place, permt[nf:, :])
        cpermt[...] = ct.astype(BF16)
        cmask[...] = RHO * (1.0 - jnp.sum(ct, axis=0, keepdims=True))

    lane = lax.broadcasted_iota(jnp.int32, (rows, 128), 1)
    inv_low = jnp.where(ix == nx - 1, 0.5, 0.25).astype(F32)
    inv_high = jnp.where(ix == 0, 0.5, 0.25).astype(F32)
    entries = ndev * ncorn

    for it in range(ITERS):
        for c in range(nch):
            if it == 0:
                flex_copy(c).wait()
            s = slice(c * cw, (c + 1) * cw)
            f = dot(loads_ref[...] if it == 0 else rhs[...], flex[:, s])
            fld[:, s] = f
            hi, lo = split(f)
            fhi[:, s] = hi
            flo[:, s] = lo
        if it == ITERS - 1:
            out_field = pltpu.make_async_copy(fld, field_out, osem.at[0])
            out_field.start()

        cs[it] = dot(fhi[...], cperm[...]) + dot(flo[...], cperm[...])
        if it == 0:
            pl.semaphore_wait(barrier, ndev - 1)
        ccopies = []
        for k, step in enumerate((-1, 1) if ny > 2 else (1,)):
            ccopies.append(pltpu.make_async_remote_copy(
                src_ref=cs.at[it], dst_ref=cr.at[it, k], send_sem=csend.at[it, k],
                recv_sem=crecv.at[it, k],
                device_id=(ix, lax.rem(iy + step + ny, ny)), device_id_type=MESH))
            ccopies[-1].start()

        def face_copy(r):
            return pltpu.make_async_remote_copy(
                src_ref=tb.at[it, r], dst_ref=rv.at[it, r], send_sem=tsend.at[it, r],
                recv_sem=trecv.at[it, r], device_id=partners[r][1], device_id_type=MESH)

        def on(r, action):
            if partners[r][0] is None:
                action(face_copy(r))
            else:
                @pl.when(partners[r][0])
                def _():
                    action(face_copy(r))

        def send_pair(p):
            base = p * pair_w
            t = dot(fhi[...], perm[:, base:base + pair_w])
            h = rows // 4
            for q in (1, 0):
                r = 2 * p + q
                tb[it, r, :rows, :] = t[:, q * 256:(q + 1) * 256].astype(BF16)
                tail = fold(t[:, 512:], q == 0).astype(BF16)
                tb[it, r, rows:, :128] = tail[:h]
                tb[it, r, rows:, 128:] = tail[h:]
                on(r, lambda c: c.start())

        for p in PAIRS:
            send_pair(p)

        for c in ccopies:
            c.wait_recv()
        own = cs[it]
        fromup, fromdown = cr[it, 0], cr[it, len(ccopies) - 1]
        w = own + jnp.where(lax.rem(lane, 64) < 32, pltpu.roll(fromup, 96, 1), pltpu.roll(fromdown, 32, 1))
        us[it, 0] = fold(w, True)
        us[it, 1] = fold(w, False)

        def side_copy(k):
            to = jnp.clip(ix + 1 if k == 0 else ix - 1, 0, nx - 1)
            return pltpu.make_async_remote_copy(
                src_ref=us.at[it, k], dst_ref=ur.at[it, k], send_sem=usend.at[it, k],
                recv_sem=urecv.at[it, k], device_id=(to, iy), device_id_type=MESH)

        @pl.when(ix < nx - 1)
        def _():
            side_copy(0).start()

        @pl.when(ix > 0)
        def _():
            side_copy(1).start()

        if it == 0:
            build_t()

        @pl.when(ix > 0)
        def _():
            side_copy(0).wait_recv()

        @pl.when(ix < nx - 1)
        def _():
            side_copy(1).wait_recv()

        cross = w + unfold(ur[it, 1], ur[it, 0])
        resid = own - cross * jnp.where(lane < 64, inv_low, inv_high)
        z = jnp.concatenate([resid * resid, jnp.zeros((256 - rows, 128), F32)], axis=0)
        part = jnp.sum(z.T, axis=0, keepdims=True)
        sq[it] = part

        def spread(k, carry):
            pltpu.make_async_remote_copy(
                src_ref=sq.at[it], dst_ref=sr.at[it, ndev - 1 - k], send_sem=ssend.at[it],
                recv_sem=srecv.at[it], device_id=peer(k), device_id_type=MESH).start()
            return carry

        lax.fori_loop(1, ndev, spread, 0)

        for c in range(nch):
            s = slice(c * cw, (c + 1) * cw)
            own_part = cmask[:, s] * fld[:, s]
            mult[:, s] = own_part if it == 0 else mult[:, s] + own_part

        def add_back(x, m):
            for c in range(nch):
                s = slice(c * cw, (c + 1) * cw)
                mult[:, s] += m(x, s)

        for p in PAIRS:
            for q in (1, 0):
                on(2 * p + q, lambda c: c.wait_recv())
            tails = []
            for q in (0, 1):
                r = 2 * p + q
                tails.append(jnp.concatenate([rv[it, r, rows:, :128], rv[it, r, rows:, 128:]], axis=0).astype(F32))
            x = jnp.concatenate(
                [rv[it, 2 * p, :rows, :], rv[it, 2 * p + 1, :rows, :], unfold(*tails).astype(BF16)], axis=1)
            base = p * pair_w
            add_back(x, lambda x, s: -RHO * dot(x, permt[base:base + pair_w, s]))

        pltpu.make_async_copy(sr.at[it], sr.at[it], srecv.at[it]).wait()
        total = part + jnp.sum(sr[it], axis=0)
        scale = RHO_CORNER / jnp.sqrt(total / entries + EPS)
        grid = jnp.broadcast_to(scale, (128, 256)).T[:rows]
        hi, lo = split(resid * grid)
        both = jnp.concatenate([hi, lo], axis=1)
        for c in range(nch):
            s = slice(c * cw, (c + 1) * cw)
            cp = cpermt[:, s]
            m = mult[:, s] + dot(both, jnp.concatenate([cp, cp], axis=0))
            mult[:, s] = m
            if it < ITERS - 1:
                rhs[:, s] = (loads_ref[:, s].astype(F32) - m).astype(BF16)

        for r in range(6):
            on(r, lambda c: c.wait_send())
        for c in ccopies:
            c.wait_send()

        @pl.when(ix < nx - 1)
        def _():
            side_copy(0).wait_send()

        @pl.when(ix > 0)
        def _():
            side_copy(1).wait_send()

        pltpu.make_async_copy(sr.at[it], sr.at[it], ssend.at[it]).wait()

    out_mult = pltpu.make_async_copy(mult, mult_out, osem.at[1])
    out_mult.start()
    out_field.wait()
    out_mult.wait()


def local(nx, ny, flexibility, loads, dof_order, coarse_ids):
    flex = flexibility[0, 0]
    load = loads[0, 0]
    order = dof_order[0]
    ids = coarse_ids[0]
    rows, n = load.shape
    corners = ids.shape[1]
    face = (n - corners) // 6
    ndev = nx * ny
    parts = []
    for p in range(3):
        a, b = 2 * p * face, (2 * p + 1) * face
        parts += [order[:, a:a + 256], order[:, b:b + 256],
                  order[:, a + 256:a + face], order[:, b + 256:b + face]]
    parts.append(order[:, 6 * face:])
    order = jnp.concatenate(parts, axis=1)
    vm = pl.BlockSpec(memory_space=pltpu.VMEM)
    hbm = pl.BlockSpec(memory_space=pl.ANY)
    sems = pltpu.SemaphoreType.DMA
    trace_rows = rows * face // 256
    ky = 2 if ny > 2 else 1
    out = jax.ShapeDtypeStruct((rows, n), F32)
    field, mult = pl.pallas_call(
        functools.partial(kernel, nx, ny),
        out_shape=(out, out),
        in_specs=[vm, vm, vm, hbm],
        out_specs=(hbm, hbm),
        scratch_shapes=[
            pltpu.VMEM((n, n), BF16), pltpu.VMEM((n, n), BF16), pltpu.VMEM((n, n), BF16),
            pltpu.VMEM((n, corners), BF16), pltpu.VMEM((corners, n), BF16),
            pltpu.VMEM((rows, n), F32), pltpu.VMEM((rows, n), BF16), pltpu.VMEM((rows, n), BF16),
            pltpu.VMEM((rows, n), BF16), pltpu.VMEM((rows, n), F32), pltpu.VMEM((1, n), F32),
            pltpu.VMEM((ITERS, 6, trace_rows, 256), BF16), pltpu.VMEM((ITERS, 6, trace_rows, 256), BF16),
            pltpu.VMEM((ITERS, rows, 128), F32), pltpu.VMEM((ITERS, ky, rows, 128), F32),
            pltpu.VMEM((ITERS, 2, rows // 2, 128), F32), pltpu.VMEM((ITERS, 2, rows // 2, 128), F32),
            pltpu.VMEM((ITERS, 1, 256), F32), pltpu.VMEM((ITERS, ndev - 1, 1, 256), F32),
            sems((4,)), sems((ITERS, 6)), sems((ITERS, 6)), sems((ITERS, ky)), sems((ITERS, ky)),
            sems((ITERS, 2)), sems((ITERS, 2)), sems((ITERS,)), sems((ITERS,)), sems((2,)),
        ],
        compiler_params=pltpu.CompilerParams(
            collective_id=0, has_side_effects=True, vmem_limit_bytes=60 * 1024 * 1024),
    )(order, ids, load, flex)
    return (field[None, None], mult[None, None])


def solution(mesh):
    nx, ny = mesh.shape["gx"], mesh.shape["gy"]
    placed = (
        P("gx", "gy", None, None),
        P("gx", "gy", None, None),
        P("gx", "gy", None),
        P("gx", "gy", None),
    )
    return jax.shard_map(
        functools.partial(local, nx, ny),
        mesh=mesh,
        in_specs=placed,
        out_specs=(P("gx", "gy", None, None), P("gx", "gy", None, None)),
        check_vma=False,
    )
```

```python
import functools
import jax
import jax.numpy as jnp
from jax import lax
from jax.experimental import pallas as pl
from jax.experimental.pallas import tpu as pltpu
from jax.sharding import PartitionSpec as P

ITERS = 2
RHO = 0.2
RHO_CORNER = 0.5
EPS = 1e-06
MESH = pl.DeviceIdType.MESH
ROUNDS = ((0, 1, 0), (0, 1, 1), (1, 1, 0), (1, 1, 1), (0, 2, 0), (0, 2, 2))
PAIRS = (2, 0, 1)
BACK = (1, 0, 2)
F32 = jnp.float32
BF16 = jnp.bfloat16


def dot(a, b):
    return jnp.dot(a, b, preferred_element_type=F32)


def dot_nt(a, b):
    return lax.dot_general(a, b, (((1,), (1,)), ((), ())), preferred_element_type=F32)


def split(x):
    hi = x.astype(BF16)
    return hi, (x - hi.astype(F32)).astype(BF16)


def fold(x, low):
    h = x.shape[0] // 2
    lane = lax.broadcasted_iota(jnp.int32, (h, 128), 1)
    top, bottom = x[:h], x[h:]
    if low:
        return jnp.where(lane < 64, top, pltpu.roll(bottom, 64, 1))
    return jnp.where(lane < 64, pltpu.roll(top, 64, 1), bottom)


def unfold(low, high):
    h = low.shape[0]
    lane = lax.broadcasted_iota(jnp.int32, (h, 128), 1)
    top = jnp.where(lane < 64, low, pltpu.roll(high, 64, 1))
    bottom = jnp.where(lane < 64, pltpu.roll(low, 64, 1), high)
    return jnp.concatenate([top, bottom], axis=0)


def kernel(nx, ny, order_ref, ids_ref, loads_ref, flex_hbm, field_out, mult_out,
           order, flex, perm, permt, cperm, cpermt, fld, fhi, flo, rhs, mult, cmask,
           tb, rv, cs, cr, us, ur, sq, sr,
           flex_sem, tsend, trecv, csend, crecv, usend, urecv, ssend, srecv, osem):
    rows, n = loads_ref.shape
    face = (n - 128) // 6
    pair_w = 2 * face
    ncorn = ids_ref.shape[1]
    nf = 6 * face
    ix, iy = lax.axis_index("gx"), lax.axis_index("gy")
    ndev = nx * ny
    me = ix * ny + iy
    nch = flex_sem.shape[0]
    cw = n // nch

    def flex_copy(c):
        s = pl.ds(c * cw, cw)
        return pltpu.make_async_copy(flex_hbm.at[:, s], flex.at[:, s], flex_sem.at[c])

    for c in range(nch):
        flex_copy(c).start()

    def peer(k):
        p = lax.rem(me + k, ndev)
        return (p // ny, lax.rem(p, ny))

    barrier = pltpu.get_barrier_semaphore()

    def greet(k, carry):
        pl.semaphore_signal(barrier, inc=1, device_id=peer(k), device_id_type=MESH)
        return carry

    lax.fori_loop(1, ndev, greet, 0)

    partners = []
    for axis, dist, off in ROUNDS:
        idx = ix if axis == 0 else iy
        count = nx if axis == 0 else ny
        lower = lax.rem((idx - off + 2 * dist) // dist, 2) == 0
        to = jnp.where(lower, idx + dist, idx - dist)
        if axis == 0:
            partners.append((jnp.logical_and(to >= 0, to < count), (jnp.clip(to, 0, count - 1), iy)))
        else:
            partners.append((None, (ix, lax.rem(to + count, count))))

    for it in range(ITERS):
        for r in range(6):
            present = partners[r][0]
            if present is not None:
                @pl.when(jnp.logical_not(present))
                def _():
                    rv[it, r] = jnp.zeros(rv.shape[2:], BF16)
        @pl.when(ix == 0)
        def _():
            ur[it, 0] = jnp.zeros(ur.shape[2:], F32)
        @pl.when(ix == nx - 1)
        def _():
            ur[it, 1] = jnp.zeros(ur.shape[2:], F32)

    for p in range(3):
        base = p * pair_w
        x = jnp.broadcast_to(order_ref[:, base:base + pair_w], (8, pair_w))
        turned = pltpu.roll(x, pair_w - 64, 1)
        low = lax.broadcasted_iota(jnp.int32, (8, 128), 1) < 64
        order[:, base:base + 256] = x[:, :256]
        order[:, base + 256:base + 512] = turned[:, 256:512]
        order[:, base + 512:base + pair_w] = jnp.where(low, x[:, 256:384], x[:, 512:])
    order[:, nf:] = jnp.broadcast_to(order_ref[:, nf:], (8, ncorn))
    step_p = 64

    def build(b, carry):
        base = pl.multiple_of(b * step_p, step_p)
        row = lax.broadcasted_iota(jnp.int32, (step_p, n), 0) + base
        perm[pl.ds(base, step_p), :] = jnp.where(row == order[0:1, :], 1.0, 0.0).astype(BF16)
        return carry

    lax.fori_loop(0, n // step_p, build, 0)
    ids = ids_ref[...]
    slot = ids // (ncorn // 4)
    moved = jnp.where(slot == 1, 2, jnp.where(slot == 2, 1, slot))
    ids = moved * (ncorn // 4) + lax.rem(ids, ncorn // 4)
    place = jnp.where(lax.broadcasted_iota(jnp.int32, (ncorn, ncorn), 0) == ids, 1.0, 0.0).astype(BF16)
    cperm[...] = dot_nt(perm[:, nf:], place).astype(BF16)

    def build_t():
        eye = (lax.broadcasted_iota(jnp.int32, (128, 128), 0)
               == lax.broadcasted_iota(jnp.int32, (128, 128), 1))

        def body(b, carry):
            base = pl.multiple_of(b * 128, 128)
            part = order[0:1, pl.ds(base, 128)].astype(F32)
            col = jnp.sum(jnp.where(eye, part, 0.0), axis=1, keepdims=True).astype(jnp.int32)
            hit = lax.broadcasted_iota(jnp.int32, (128, n), 1) == col
            permt[pl.ds(base, 128), :] = jnp.where(hit, 1.0, 0.0).astype(BF16)
            return carry

        lax.fori_loop(0, n // 128, body, 0)
        ct = dot(place, permt[nf:, :])
        cpermt[...] = ct.astype(BF16)
        cmask[...] = RHO * (1.0 - jnp.sum(ct, axis=0, keepdims=True))

    lane = lax.broadcasted_iota(jnp.int32, (rows, 128), 1)
    inv_low = jnp.where(ix == nx - 1, 0.5, 0.25).astype(F32)
    inv_high = jnp.where(ix == 0, 0.5, 0.25).astype(F32)
    entries = ndev * ncorn

    for it in range(ITERS):
        for c in range(nch):
            if it == 0:
                flex_copy(c).wait()
            s = slice(c * cw, (c + 1) * cw)
            f = dot(loads_ref[...] if it == 0 else rhs[...], flex[:, s])
            fld[:, s] = f
            hi, lo = split(f)
            fhi[:, s] = hi
            flo[:, s] = lo
        if it == ITERS - 1:
            out_field = pltpu.make_async_copy(fld, field_out, osem.at[0])
            out_field.start()

        cs[it] = dot(fhi[...], cperm[...]) + dot(flo[...], cperm[...])
        if it == 0:
            pl.semaphore_wait(barrier, ndev - 1)
        ccopies = []
        for k, step in enumerate((-1, 1) if ny > 2 else (1,)):
            ccopies.append(pltpu.make_async_remote_copy(
                src_ref=cs.at[it], dst_ref=cr.at[it, k], send_sem=csend.at[it, k],
                recv_sem=crecv.at[it, k],
                device_id=(ix, lax.rem(iy + step + ny, ny)), device_id_type=MESH))
            ccopies[-1].start()

        def face_copy(r):
            return pltpu.make_async_remote_copy(
                src_ref=tb.at[it, r], dst_ref=rv.at[it, r], send_sem=tsend.at[it, r],
                recv_sem=trecv.at[it, r], device_id=partners[r][1], device_id_type=MESH)

        def on(r, action):
            if partners[r][0] is None:
                action(face_copy(r))
            else:
                @pl.when(partners[r][0])
                def _():
                    action(face_copy(r))

        def send_pair(p):
            base = p * pair_w
            t = dot(fhi[...], perm[:, base:base + pair_w])
            h = rows // 4
            for q in (1, 0):
                r = 2 * p + q
                tb[it, r, :rows, :] = t[:, q * 256:(q + 1) * 256].astype(BF16)
                tail = fold(t[:, 512:], q == 0).astype(BF16)
                tb[it, r, rows:, :128] = tail[:h]
                tb[it, r, rows:, 128:] = tail[h:]
                on(r, lambda c: c.start())

        for p in PAIRS:
            send_pair(p)

        for c in ccopies:
            c.wait_recv()
        own = cs[it]
        fromup, fromdown = cr[it, 0], cr[it, len(ccopies) - 1]
        w = own + jnp.where(lax.rem(lane, 64) < 32, pltpu.roll(fromup, 96, 1), pltpu.roll(fromdown, 32, 1))
        us[it, 0] = fold(w, True)
        us[it, 1] = fold(w, False)

        def side_copy(k):
            to = jnp.clip(ix + 1 if k == 0 else ix - 1, 0, nx - 1)
            return pltpu.make_async_remote_copy(
                src_ref=us.at[it, k], dst_ref=ur.at[it, k], send_sem=usend.at[it, k],
                recv_sem=urecv.at[it, k], device_id=(to, iy), device_id_type=MESH)

        @pl.when(ix < nx - 1)
        def _():
            side_copy(0).start()

        @pl.when(ix > 0)
        def _():
            side_copy(1).start()

        if it == 0:
            build_t()

        for c in range(nch):
            s = slice(c * cw, (c + 1) * cw)
            own_part = cmask[:, s] * fld[:, s]
            mult[:, s] = own_part if it == 0 else mult[:, s] + own_part

        @pl.when(ix > 0)
        def _():
            side_copy(0).wait_recv()

        @pl.when(ix < nx - 1)
        def _():
            side_copy(1).wait_recv()

        cross = w + unfold(ur[it, 1], ur[it, 0])
        resid = own - cross * jnp.where(lane < 64, inv_low, inv_high)
        z = jnp.concatenate([resid * resid, jnp.zeros((256 - rows, 128), F32)], axis=0)
        part = jnp.sum(z.T, axis=0, keepdims=True)
        sq[it] = part

        def spread(k, carry):
            pltpu.make_async_remote_copy(
                src_ref=sq.at[it], dst_ref=sr.at[it, ndev - 1 - k], send_sem=ssend.at[it],
                recv_sem=srecv.at[it], device_id=peer(k), device_id_type=MESH).start()
            return carry

        lax.fori_loop(1, ndev, spread, 0)

        def add_back(x, m):
            for c in range(nch):
                s = slice(c * cw, (c + 1) * cw)
                mult[:, s] += m(x, s)

        for p in BACK:
            for q in (1, 0):
                on(2 * p + q, lambda c: c.wait_recv())
            tails = []
            for q in (0, 1):
                r = 2 * p + q
                tails.append(jnp.concatenate([rv[it, r, rows:, :128], rv[it, r, rows:, 128:]], axis=0).astype(F32))
            x = jnp.concatenate(
                [rv[it, 2 * p, :rows, :], rv[it, 2 * p + 1, :rows, :], unfold(*tails).astype(BF16)], axis=1)
            base = p * pair_w
            add_back(x, lambda x, s: -RHO * dot(x, permt[base:base + pair_w, s]))

        pltpu.make_async_copy(sr.at[it], sr.at[it], srecv.at[it]).wait()
        total = part + jnp.sum(sr[it], axis=0)
        scale = RHO_CORNER / jnp.sqrt(total / entries + EPS)
        grid = jnp.broadcast_to(scale, (128, 256)).T[:rows]
        hi, lo = split(resid * grid)
        both = jnp.concatenate([hi, lo], axis=1)
        for c in range(nch):
            s = slice(c * cw, (c + 1) * cw)
            cp = cpermt[:, s]
            m = mult[:, s] + dot(both, jnp.concatenate([cp, cp], axis=0))
            mult[:, s] = m
            if it < ITERS - 1:
                rhs[:, s] = (loads_ref[:, s].astype(F32) - m).astype(BF16)

        for r in range(6):
            on(r, lambda c: c.wait_send())
        for c in ccopies:
            c.wait_send()

        @pl.when(ix < nx - 1)
        def _():
            side_copy(0).wait_send()

        @pl.when(ix > 0)
        def _():
            side_copy(1).wait_send()

        pltpu.make_async_copy(sr.at[it], sr.at[it], ssend.at[it]).wait()

    out_mult = pltpu.make_async_copy(mult, mult_out, osem.at[1])
    out_mult.start()
    out_field.wait()
    out_mult.wait()


def local(nx, ny, flexibility, loads, dof_order, coarse_ids):
    flex = flexibility[0, 0]
    load = loads[0, 0]
    ids = coarse_ids[0]
    rows, n = load.shape
    corners = ids.shape[1]
    face = (n - corners) // 6
    ndev = nx * ny
    vm = pl.BlockSpec(memory_space=pltpu.VMEM)
    hbm = pl.BlockSpec(memory_space=pl.ANY)
    sems = pltpu.SemaphoreType.DMA
    trace_rows = rows * face // 256
    ky = 2 if ny > 2 else 1
    out = jax.ShapeDtypeStruct((rows, n), F32)
    field, mult = pl.pallas_call(
        functools.partial(kernel, nx, ny),
        out_shape=(out, out),
        in_specs=[vm, vm, vm, hbm],
        out_specs=(hbm, hbm),
        scratch_shapes=[
            pltpu.VMEM((8, n), jnp.int32),
            pltpu.VMEM((n, n), BF16), pltpu.VMEM((n, n), BF16), pltpu.VMEM((n, n), BF16),
            pltpu.VMEM((n, corners), BF16), pltpu.VMEM((corners, n), BF16),
            pltpu.VMEM((rows, n), F32), pltpu.VMEM((rows, n), BF16), pltpu.VMEM((rows, n), BF16),
            pltpu.VMEM((rows, n), BF16), pltpu.VMEM((rows, n), F32), pltpu.VMEM((1, n), F32),
            pltpu.VMEM((ITERS, 6, trace_rows, 256), BF16), pltpu.VMEM((ITERS, 6, trace_rows, 256), BF16),
            pltpu.VMEM((ITERS, rows, 128), F32), pltpu.VMEM((ITERS, ky, rows, 128), F32),
            pltpu.VMEM((ITERS, 2, rows // 2, 128), F32), pltpu.VMEM((ITERS, 2, rows // 2, 128), F32),
            pltpu.VMEM((ITERS, 1, 256), F32), pltpu.VMEM((ITERS, ndev - 1, 1, 256), F32),
            sems((4,)), sems((ITERS, 6)), sems((ITERS, 6)), sems((ITERS, ky)), sems((ITERS, ky)),
            sems((ITERS, 2)), sems((ITERS, 2)), sems((ITERS,)), sems((ITERS,)), sems((2,)),
        ],
        compiler_params=pltpu.CompilerParams(
            collective_id=0, has_side_effects=True, vmem_limit_bytes=44 * 1024 * 1024),
    )(dof_order[0], ids, load, flex)
    return (field[None, None], mult[None, None])


def solution(mesh):
    nx, ny = mesh.shape["gx"], mesh.shape["gy"]
    placed = (
        P("gx", "gy", None, None),
        P("gx", "gy", None, None),
        P("gx", "gy", None),
        P("gx", "gy", None),
    )
    return jax.shard_map(
        functools.partial(local, nx, ny),
        mesh=mesh,
        in_specs=placed,
        out_specs=(P("gx", "gy", None, None), P("gx", "gy", None, None)),
        check_vma=False,
    )
```
